768 devices in a mesh: dp: 96 (over y, z_lo, core), ctx: 8 (over x, z_hi).
Axes of the slice: x: 4, y: 8, z: 12 (z_hi: 2, z_lo: 6; z = z_hi * 6 + z_lo), core: 2. Of those that a mesh axis runs over, the one named last changes fastest.
Arguments:
- inputs: bfloat16 [96, 1024, 9216], P('dp', 'ctx'), may hold values from -6 to 6
- block_order: int32 [16], replicated, may hold values from 0 to 15, each once
- w_value: bfloat16 [9216, 128], P('dp'), may hold values from -0.0625 to 0.0625
- query: bfloat16 [96, 1024, 2048], P('dp', 'ctx'), may hold values from -6 to 6
- keys: bfloat16 [96, 1024, 128], P('dp', 'ctx'), may hold values from -6 to 6
- out_grad: bfloat16 [96, 1024, 2048], P('dp', 'ctx'), may hold values from -6 to 6
Outputs:
- attn_out: bfloat16 [96, 1024, 2048], P('dp', 'ctx')
- grad_query: bfloat16 [96, 1024, 2048], P('dp', 'ctx')
- grad_keys: bfloat16 [96, 1024, 128], P('dp', 'ctx')
- grad_w: float32 [9216, 128], P('dp')
The draws below stay inside these ranges and needn't reach their ends.
Inputs may be any that keep to these rules, and one draw needn't show every extreme that they name: `block_order`: a permutation of the block numbers.
All inputs are finite; a program needn't handle non-finite values.
Results may differ from the reference program's by a relative error of at most 0.02.
Values may be sent and summed in bfloat16 or wider, within the bound.
No kernel may reach another device: no remote copies, remote signals or barrier semaphores. Data moves between devices by JAX's collectives and lax.ppermute only.
A program may use at most 64 MiB of HBM per device.

```python
import jax
import jax.numpy as jnp
from jax import lax

D = 9216
HD = 128
HQ = 16
BLK = 64
N_BLOCKS = 16
SEQ = 1024
N_DP = 96
N_CTX = 8


def draw_keys(key, part):
    noise_key = jax.random.fold_in(key, 77)
    field = jnp.clip(jax.random.normal(noise_key, (N_DP, SEQ, HD)), -6.0, 6.0)
    return field.astype(jnp.bfloat16)


def draw_query(key, part):
    noise_key = jax.random.fold_in(key, 91)
    field = jnp.clip(jax.random.normal(noise_key, (N_DP, SEQ, HQ, HD)), -6.0, 6.0)
    return field.reshape(N_DP, SEQ, HQ * HD).astype(jnp.bfloat16)


def steps_of(key, extent, shards, least, top_value):
    factor_of = 1.0
    for dim, shards_of in shards:
        steps = jax.random.uniform(jax.random.fold_in(jax.random.fold_in(key, 6), dim), (shards_of,), jnp.float32, least / len(shards), top_value / len(shards))
        factor_of = factor_of * jnp.repeat(jnp.exp(steps), extent[dim] // shards_of).reshape((-1,) + (1,) * (len(extent) - 1 - dim))
    return factor_of


def scatter_about(key, dims, spread, most, cuts=(), kind=jnp.bfloat16):
    factor_of = steps_of(key, dims, cuts, -0.22, 0.18) if cuts else 1.0
    array = jax.random.normal(key, dims, jnp.float32) * spread * factor_of
    return jnp.minimum(jnp.maximum(array, -most), most).astype(kind)


def setup_inputs(seed: int = 0) -> dict:
    seeds = jax.random.split(jax.random.key(seed), 7)
    inputs = scatter_about(seeds[0], (N_DP, SEQ, D), 1.0, 6.0, ((0, 96), (1, 8)))
    block_order = jax.random.permutation(seeds[1], N_BLOCKS).astype(jnp.int32)
    w_value = scatter_about(seeds[2], (D, HD), D ** -0.5, 0.0625, ((0, 96),))
    query = draw_query(jax.random.fold_in(seeds[6], 71), 0)
    keys = draw_keys(jax.random.fold_in(seeds[6], 71), 0)
    out_grad = scatter_about(seeds[5], (N_DP, SEQ, HQ * HD), 1.0, 6.0, ((0, 96), (1, 8)))
    return {"inputs": inputs, "block_order": block_order, "w_value": w_value, "query": query, "keys": keys, "out_grad": out_grad}


def reference(inputs, block_order, w_value, query, keys, out_grad):
    held = jnp.arange(SEQ, dtype=jnp.int32)
    place = (block_order[held // BLK] * BLK + held % BLK).astype(jnp.int32)
    place_groups = place.reshape(N_CTX, 2 * BLK)
    place_before = jnp.roll(place_groups, 1, axis=0)
    scale = 1.0 / (HD ** 0.5)

    def window(packed):
        q_group, k_group, v_group, g_group, k_before, v_before, p_group, p_before = packed
        all_keys = jnp.concatenate([k_group, k_before], axis=0)
        all_values = jnp.concatenate([v_group, v_before], axis=0)
        key_place = jnp.concatenate([p_group, p_before], axis=0)
        allowed = key_place[None, :] <= p_group[:, None]
        q_flat = q_group.reshape(2 * BLK * HQ, HD)
        g_flat = g_group.reshape(2 * BLK * HQ, HD)
        scores = jnp.dot(q_flat, all_keys.T, preferred_element_type=jnp.float32) * scale
        scores = scores.reshape(2 * BLK, HQ, 4 * BLK)
        scores = jnp.where(allowed[:, None, :], scores, -1e30)
        top = jnp.max(scores, axis=2, keepdims=True)
        weights = jnp.exp(scores - top)
        prob = (weights / jnp.sum(weights, axis=2, keepdims=True)).reshape(2 * BLK * HQ, 4 * BLK)
        prob_b = prob.astype(jnp.bfloat16)
        result = jnp.dot(prob_b, all_values, preferred_element_type=jnp.float32).astype(jnp.bfloat16)
        delta = jnp.sum(g_flat.astype(jnp.float32) * result.astype(jnp.float32), axis=1, keepdims=True)
        dprob = jnp.dot(g_flat, all_values.T, preferred_element_type=jnp.float32)
        dscore = (prob * (dprob - delta)).astype(jnp.bfloat16)
        dquery = (jnp.dot(dscore, all_keys, preferred_element_type=jnp.float32) * scale).astype(jnp.bfloat16)
        dkeys_pair = jnp.dot(dscore.T, q_flat, preferred_element_type=jnp.float32) * scale
        dvalues_pair = jnp.dot(prob_b.T, g_flat, preferred_element_type=jnp.float32)
        return (result.reshape(2 * BLK, HQ * HD), dquery.reshape(2 * BLK, HQ * HD), dkeys_pair, dvalues_pair)

    def one(total, packed):
        x_rows, q_rows, k_rows, grad_rows = packed
        values = jnp.dot(x_rows, w_value, preferred_element_type=jnp.float32).astype(jnp.bfloat16)
        q_groups = q_rows.reshape(N_CTX, 2 * BLK, HQ * HD)
        g_groups = grad_rows.reshape(N_CTX, 2 * BLK, HQ * HD)
        k_groups = k_rows.reshape(N_CTX, 2 * BLK, HD)
        v_groups = values.reshape(N_CTX, 2 * BLK, HD)
        result, dquery, dkeys_pair, dvalues_pair = lax.map(
            window,
            (q_groups, k_groups, v_groups, g_groups, jnp.roll(k_groups, 1, axis=0),
             jnp.roll(v_groups, 1, axis=0), place_groups, place_before))
        dkeys = dkeys_pair[:, :2 * BLK] + jnp.roll(dkeys_pair[:, 2 * BLK:], -1, axis=0)
        dvalues = dvalues_pair[:, :2 * BLK] + jnp.roll(dvalues_pair[:, 2 * BLK:], -1, axis=0)
        dkeys = dkeys.astype(jnp.bfloat16).reshape(SEQ, HD)
        dvalues = dvalues.astype(jnp.bfloat16).reshape(SEQ, HD)
        total = total + jnp.dot(x_rows.T, dvalues, preferred_element_type=jnp.float32)
        return total, (result.reshape(SEQ, HQ * HD), dquery.reshape(SEQ, HQ * HD), dkeys)

    start = jnp.zeros((D, HD), jnp.float32)
    grad_w, outs = lax.scan(one, start, (inputs, query, keys, out_grad))
    return outs[0], outs[1], outs[2], grad_w
```

```python
import jax
import jax.numpy as jnp
from jax import lax
from jax.sharding import Mesh
from jax.sharding import PartitionSpec as P

BLK = 64
NY, NZ, NC, NX, NH = 8, 6, 2, 4, 2
DP = ("y", "zl", "c")
CTX = ("x", "zh")
BF = jnp.bfloat16
F32 = jnp.float32


def shifted(value, axis, steps):
    count = lax.axis_size(axis)
    pairs = [(source, (source + steps) % count) for source in range(count)]
    return lax.ppermute(value, axis, pairs)


def exchanged(value, axis):
    return lax.all_to_all(value, axis, 0, 0, tiled=True)


def gathered_weight(w):
    part = w.shape[0] // NX
    xi = lax.axis_index("x")
    piece = lax.dynamic_slice_in_dim(w, part * xi, part, 0)
    own = exchanged(jnp.broadcast_to(piece[None], (NY * NZ,) + piece.shape), ("y", "zl"))
    left = shifted(own, "x", 1)
    right = shifted(own, "x", -1)
    half = NY * NZ // 2
    far = jnp.concatenate([shifted(left[:half], "x", 1), shifted(right[half:], "x", -1)], axis=0)
    turn = jnp.stack([own, right, far, left, own, right, far], axis=0)
    mine = lax.dynamic_slice_in_dim(turn, (NX - xi) % NX, NX, 0)
    theirs = shifted(mine, "c", 1)
    first = lax.axis_index("c") == 0
    both = jnp.stack([jnp.where(first, mine, theirs), jnp.where(first, theirs, mine)], axis=0)
    return both.transpose(2, 0, 1, 3, 4).reshape(NY * NZ * NC * NX * part, w.shape[1])


def scattered_sum(term):
    part = term.shape[0] // (NY * NZ * NC * NX)
    hd = term.shape[1]
    blocks = term.reshape(NY * NZ, NC, NX, part, hd)
    ci = lax.axis_index("c")
    mine = lax.dynamic_index_in_dim(blocks, ci, 1, keepdims=False)
    theirs = lax.dynamic_index_in_dim(blocks, 1 - ci, 1, keepdims=False).astype(BF)
    total = mine + shifted(theirs, "c", 1).astype(F32)
    sent = total.astype(BF).transpose(1, 0, 2, 3)
    total = jnp.sum(exchanged(sent, "x").astype(F32), axis=0)
    sent = total.astype(BF).reshape(NY, NZ, part, hd)
    total = jnp.sum(exchanged(sent, "y").astype(F32), axis=0)
    sent = total.astype(BF)[:, None]
    sent = jnp.broadcast_to(sent, (NZ, NH, part, hd)).reshape(NZ * NH, part, hd)
    total = jnp.sum(exchanged(sent, ("zl", "zh")).astype(F32), axis=0)
    sent = jnp.broadcast_to(total.astype(BF)[None], (NX, part, hd))
    return exchanged(sent, "x").reshape(NX * part, hd).astype(F32)


def shards(inputs, block_order, w_value, query, keys, out_grad):
    x_rows = inputs[0]
    q_rows = query[0]
    k_rows = keys[0]
    grad_rows = out_grad[0]
    rows = x_rows.shape[0]
    head_size = k_rows.shape[1]
    head_count = q_rows.shape[1] // head_size
    scale = 1.0 / head_size**0.5
    far_keys = shifted(k_rows, CTX, 1)
    w_full = gathered_weight(w_value)

    index = lax.axis_index(CTX)
    count = lax.axis_size(CTX)
    before = (index + count - 1) % count
    local_iota = jnp.arange(rows, dtype=jnp.int32)

    def places(owner):
        slots = lax.dynamic_slice_in_dim(block_order, 2 * owner, 2, 0)
        return slots[local_iota // BLK] * BLK + local_iota % BLK

    mine = places(index)
    theirs = places(before)
    key_place = jnp.concatenate([mine, theirs], axis=0)
    allowed = key_place[None, :] <= mine[:, None]
    all_keys = jnp.concatenate([k_rows, far_keys], axis=0)
    q_flat = q_rows.reshape(rows * head_count, head_size)
    g_flat = grad_rows.reshape(rows * head_count, head_size)
    scores = jnp.dot(q_flat, all_keys.T, preferred_element_type=F32) * scale
    scores = scores.reshape(rows, head_count, 2 * rows)
    scores = jnp.where(allowed[:, None, :], scores, -1e30)
    top = jnp.max(scores, axis=2, keepdims=True)
    weights = jnp.exp(scores - top)
    prob = (weights / jnp.sum(weights, axis=2, keepdims=True)).reshape(rows * head_count, 2 * rows)
    prob_b = prob.astype(BF)
    dvalues_all = jnp.dot(prob_b.T, g_flat, preferred_element_type=F32)
    back_values = shifted(dvalues_all[rows:].astype(BF), CTX, -1).astype(F32)
    dvalues = (dvalues_all[:rows] + back_values).astype(BF)
    term = jnp.dot(x_rows.T, dvalues, preferred_element_type=F32)
    grad_w = scattered_sum(term)

    values = jnp.dot(x_rows, w_full, preferred_element_type=F32).astype(BF)
    far_values = shifted(values, CTX, 1)
    all_values = jnp.concatenate([values, far_values], axis=0)
    result = jnp.dot(prob_b, all_values, preferred_element_type=F32).astype(BF)
    delta = jnp.sum(g_flat.astype(F32) * result.astype(F32), axis=1, keepdims=True)
    dprob = jnp.dot(g_flat, all_values.T, preferred_element_type=F32)
    dscore = (prob * (dprob - delta)).astype(BF)
    dquery = (jnp.dot(dscore, all_keys, preferred_element_type=F32) * scale).astype(BF)
    dkeys_all = jnp.dot(dscore.T, q_flat, preferred_element_type=F32) * scale
    back_keys = shifted(dkeys_all[rows:].astype(BF), CTX, -1).astype(F32)
    dkeys = (dkeys_all[:rows] + back_keys).astype(BF)
    attn_rows = result.reshape(rows, head_count * head_size)
    query_grads = dquery.reshape(rows, head_count * head_size)
    return (attn_rows[None], query_grads[None], dkeys[None], grad_w)


def solution(mesh):
    fine = Mesh(mesh.devices.reshape(NY, NZ, NC, NX, NH), ("y", "zl", "c", "x", "zh"))
    return jax.shard_map(
        shards,
        mesh=fine,
        in_specs=(
            P(DP, CTX, None),
            P(),
            P(DP, None),
            P(DP, CTX, None),
            P(DP, CTX, None),
            P(DP, CTX, None),
        ),
        out_specs=(P(DP, CTX, None), P(DP, CTX, None), P(DP, CTX, None), P(DP, None)),
        check_vma=False,
    )
```

```python
import functools

import jax
import jax.numpy as jnp
from jax import lax
from jax.experimental import pallas as pl
from jax.experimental.pallas import tpu as pltpu
from jax.sharding import Mesh
from jax.sharding import PartitionSpec as P

BLK = 64
NY, NZ, NC, NX, NH = 8, 6, 2, 4, 2
DP = ("y", "zl", "c")
CTX = ("x", "zh")
BF = jnp.bfloat16
F32 = jnp.float32
VM = pl.BlockSpec(memory_space=pltpu.VMEM)
SM = pl.BlockSpec(memory_space=pltpu.SMEM)


def in_hbm(value):
    return pltpu.with_memory_space_constraint(value, pltpu.HBM)


def shifted(value, axis, steps):
    count = lax.axis_size(axis)
    pairs = [(source, (source + steps) % count) for source in range(count)]
    return lax.ppermute(value, axis, pairs)


def exchanged(value, axis):
    return lax.all_to_all(value, axis, 0, 0, tiled=True)


def kernel(body, ins, outs, flops, limit=24 * 2**20):
    size = sum(o.size * o.dtype.itemsize for o in outs)
    return pl.pallas_call(
        body,
        out_shape=outs,
        in_specs=ins,
        out_specs=[VM] * len(outs),
        cost_estimate=pl.CostEstimate(flops=flops, bytes_accessed=2 * size, transcendentals=0),
        compiler_params=pltpu.CompilerParams(vmem_limit_bytes=limit),
    )


def dot(a, b, ca, cb):
    return lax.dot_general(a, b, (((ca,), (cb,)), ((), ())), preferred_element_type=F32)


def places(order, owner, shape, axis):
    at = lax.broadcasted_iota(jnp.int32, shape, axis)
    low, high = order[2 * owner], order[2 * owner + 1]
    return jnp.where(at < BLK, low * BLK + at, (high - 1) * BLK + at)


def prob_body(heads, scale, order, who, q, g, k, k_far, prob, near, far):
    rows, hd = k.shape
    all_keys = jnp.concatenate([k[...], k_far[...]], axis=0)
    mine = places(order, who[0], (rows, rows), 0)
    here = places(order, who[0], (rows, rows), 1)
    back = places(order, who[1], (rows, rows), 1)
    allowed = jnp.concatenate([here <= mine, back <= mine], axis=1)
    total = jnp.zeros((2 * rows, hd), F32)
    for h in range(heads):
        cols = slice(h * hd, (h + 1) * hd)
        scores = jnp.where(allowed, dot(q[:, cols], all_keys, 1, 1) * scale, -1e30)
        weights = jnp.exp(scores - jnp.max(scores, axis=1, keepdims=True))
        p = (weights * (1.0 / jnp.sum(weights, axis=1, keepdims=True))).astype(BF)
        prob[h] = p
        total += dot(p, g[:, cols], 0, 0)
    near[...] = total[:rows]
    far[...] = total[rows:].astype(BF)


def back_body(heads, scale, prob, q, g, k, k_far, v, v_far, attn, dq, near, far):
    rows, hd = k.shape
    all_keys = jnp.concatenate([k[...], k_far[...]], axis=0)
    all_values = jnp.concatenate([v[...], v_far[...]], axis=0)
    total = jnp.zeros((2 * rows, hd), F32)
    for h in range(heads):
        cols = slice(h * hd, (h + 1) * hd)
        p = prob[h]
        gh = g[:, cols]
        out = dot(p, all_values, 1, 0).astype(BF)
        attn[:, cols] = out
        delta = jnp.sum(gh.astype(F32) * out.astype(F32), axis=1, keepdims=True)
        ds = (p.astype(F32) * (dot(gh, all_values, 1, 1) - delta)).astype(BF)
        dq[:, cols] = (dot(ds, all_keys, 1, 0) * scale).astype(BF)
        total += dot(ds, q[:, cols], 0, 0)
    near[...] = total[:rows] * scale
    far[...] = (total[rows:] * scale).astype(BF)


def term_body(part, who, x, near, back, mine, theirs):
    dv = (near[...] + back[...].astype(F32)).astype(BF)
    first = who[2] == 0
    group = NC * NX * part
    step = 2 * group
    for j in range(x.shape[1] // step):
        t = dot(x[:, j * step : (j + 1) * step], dv, 0, 0)
        at = slice(2 * part * j, 2 * part * (j + 1))
        for quarter in range(NX):

            def rows_of(c):
                low = c * NX * part + quarter * part
                return jnp.concatenate([t[low : low + part], t[group + low : group + low + part]], axis=0)

            zero, one = rows_of(0), rows_of(1)
            mine[quarter, at] = jnp.where(first, zero, one).astype(BF)
            theirs[quarter, at] = jnp.where(first, one, zero).astype(BF)


def quarter_of(who, step, mine, theirs):
    at = lax.rem(who[3] + step, NX)
    return mine[at].astype(F32) + theirs[at].astype(F32)


def far_body(who, mine, theirs, low, high):
    half = low.shape[0]
    far = quarter_of(who, 2, mine, theirs).astype(BF)
    low[...] = far[:half]
    high[...] = far[half:]


def side_body(who, mine, theirs, low, high, right, left):
    half = low.shape[0]
    one = quarter_of(who, 1, mine, theirs)
    right[:half] = (one[:half] + low[...].astype(F32)).astype(BF)
    right[half:] = one[half:].astype(BF)
    one = quarter_of(who, 3, mine, theirs)
    left[:half] = one[:half].astype(BF)
    left[half:] = (one[half:] + high[...].astype(F32)).astype(BF)


def own_body(who, mine, theirs, right, left, out):
    total = quarter_of(who, 0, mine, theirs) + right[...].astype(F32) + left[...].astype(F32)
    out[...] = total.astype(BF)


def sum_body(copies, parts, out):
    total = parts[0].astype(F32)
    for i in range(1, parts.shape[0]):
        total += parts[i].astype(F32)
    total = total.astype(BF)
    if copies == 0:
        out[...] = total
    else:
        for i in range(copies):
            out[:, i] = total


def summed(parts, copies):
    shape = parts.shape[1:]
    if copies:
        shape = (shape[0], copies) + shape[1:]
    out = jax.ShapeDtypeStruct(shape, BF)
    return kernel(functools.partial(sum_body, copies), [VM], [out], parts.size)(parts)[0]


def gathered_weight(w):
    def everywhere(block, axis):
        count = lax.axis_size(axis)
        return exchanged(jnp.broadcast_to(block[None], (count,) + block.shape), axis)

    own = everywhere(w, "zl")
    mine = everywhere(own, "y").reshape((NY * NZ,) + w.shape)
    theirs = shifted(mine, "c", 1)
    first = lax.axis_index("c") == 0
    both = jnp.stack([jnp.where(first, mine, theirs), jnp.where(first, theirs, mine)], axis=1)
    return both.reshape(NY * NZ * NC * w.shape[0], w.shape[1])


def scattered_sum(who, x_rows, near, back, part):
    rows, width = x_rows.shape
    hd = near.shape[1]
    full = (NX, NY * NZ * part, hd)
    mine, theirs = kernel(
        functools.partial(term_body, part),
        [SM, VM, VM, VM],
        [jax.ShapeDtypeStruct(full, BF)] * 2,
        2 * rows * width * hd,
    )(who, x_rows, near, back)
    theirs = shifted(theirs, "c", 1)
    size = NY * NZ * part
    quarter = jax.ShapeDtypeStruct((size, hd), BF)
    half = jax.ShapeDtypeStruct((size // 2, hd), BF)
    low, high = kernel(far_body, [SM, VM, VM], [half] * 2, size * hd)(who, mine, theirs)
    low = shifted(low, "x", 1)
    high = shifted(high, "x", -1)
    right, left = kernel(side_body, [SM] + [VM] * 4, [quarter] * 2, 2 * size * hd)(who, mine, theirs, low, high)
    right = shifted(right, "x", 1)
    left = shifted(left, "x", -1)
    total = kernel(own_body, [SM] + [VM] * 4, [quarter], size * hd)(who, mine, theirs, right, left)[0]
    total = total.reshape(NY, NZ, part, hd)
    got = exchanged(total, "y")
    total = summed(got, NH).reshape(NZ * NH, part, hd)
    got = exchanged(total, ("zl", "zh"))
    total = summed(got[:, None], NX)[0]
    return exchanged(total, "x").reshape(NX * part, hd).astype(F32)


def shards(inputs, block_order, w_value, query, keys, out_grad):
    x_rows = inputs[0]
    q_rows = query[0]
    k_rows = keys[0]
    grad_rows = out_grad[0]
    rows, hd = k_rows.shape
    heads = q_rows.shape[1] // hd
    scale = 1.0 / hd**0.5
    index = lax.axis_index(CTX)
    count = lax.axis_size(CTX)
    who = jnp.stack([index, (index + count - 1) % count, lax.axis_index("c"), lax.axis_index("x")]).astype(jnp.int32)
    block = jax.ShapeDtypeStruct((rows, hd), F32)
    block_b = jax.ShapeDtypeStruct((rows, hd), BF)
    wide_b = jax.ShapeDtypeStruct(q_rows.shape, BF)
    work = 2 * rows * 2 * rows * hd * heads

    far_keys = shifted(k_rows, CTX, 1)
    w_full = gathered_weight(w_value)

    prob, near, far = kernel(
        functools.partial(prob_body, heads, scale),
        [SM, SM, VM, VM, VM, VM],
        [jax.ShapeDtypeStruct((heads, rows, 2 * rows), BF), block, block_b],
        4 * work,
    )(in_hbm(block_order), who, in_hbm(q_rows), in_hbm(grad_rows), in_hbm(k_rows), far_keys)
    back = shifted(far, CTX, -1)
    grad_w = scattered_sum(who, x_rows, near, back, w_value.shape[0] // NX)

    values = jnp.dot(x_rows, w_full, preferred_element_type=F32).astype(BF)
    far_values = shifted(values, CTX, 1)
    attn, dquery, near_k, far_k = kernel(
        functools.partial(back_body, heads, scale),
        [VM] * 7,
        [wide_b, wide_b, block, block_b],
        6 * work,
    )(prob, q_rows, grad_rows, k_rows, far_keys, values, far_values)
    back_keys = shifted(far_k, CTX, -1).astype(F32)
    dkeys = (near_k + back_keys).astype(BF)
    return (attn[None], dquery[None], dkeys[None], grad_w)


def solution(mesh):
    fine = Mesh(mesh.devices.reshape(NY, NZ, NC, NX, NH), ("y", "zl", "c", "x", "zh"))
    return jax.shard_map(
        shards,
        mesh=fine,
        in_specs=(
            P(DP, CTX, None),
            P(),
            P(DP, None),
            P(DP, CTX, None),
            P(DP, CTX, None),
            P(DP, CTX, None),
        ),
        out_specs=(P(DP, CTX, None), P(DP, CTX, None), P(DP, CTX, None), P(DP, None)),
        check_vma=False,
    )
```

```python
import functools

import jax
import jax.numpy as jnp
from jax import lax
from jax.experimental import pallas as pl
from jax.experimental.pallas import tpu as pltpu
from jax.sharding import Mesh
from jax.sharding import PartitionSpec as P

BLK = 64
NY, NZ, NC, NX, NH = 8, 6, 2, 4, 2
DP = ("y", "zl", "c")
CTX = ("x", "zh")
BF = jnp.bfloat16
F32 = jnp.float32
VM = pl.BlockSpec(memory_space=pltpu.VMEM)
SM = pl.BlockSpec(memory_space=pltpu.SMEM)


def in_hbm(value):
    return pltpu.with_memory_space_constraint(value, pltpu.HBM)


def shifted(value, axis, steps):
    count = lax.axis_size(axis)
    pairs = [(source, (source + steps) % count) for source in range(count)]
    return lax.ppermute(value, axis, pairs)


def exchanged(value, axis):
    return lax.all_to_all(value, axis, 0, 0, tiled=True)


def kernel(body, ins, outs, flops):
    size = sum(o.size * o.dtype.itemsize for o in outs)
    return pl.pallas_call(
        body,
        out_shape=outs,
        in_specs=ins,
        out_specs=[VM] * len(outs),
        cost_estimate=pl.CostEstimate(flops=flops, bytes_accessed=2 * size, transcendentals=0),
        compiler_params=pltpu.CompilerParams(vmem_limit_bytes=24 * 2**20),
    )


def dot(a, b, ca, cb):
    return lax.dot_general(a, b, (((ca,), (cb,)), ((), ())), preferred_element_type=F32)


def places(order, owner, shape, axis):
    at = lax.broadcasted_iota(jnp.int32, shape, axis)
    low, high = order[2 * owner], order[2 * owner + 1]
    return jnp.where(at < BLK, low * BLK + at, (high - 1) * BLK + at)


def probabilities(scale, order, who, k, k_far):
    rows = k.shape[0]
    all_keys = jnp.concatenate([k[...], k_far[...]], axis=0)
    mine = places(order, who[0], (rows, rows), 0)
    here = places(order, who[0], (rows, rows), 1)
    back = places(order, who[1], (rows, rows), 1)
    allowed = jnp.concatenate([here <= mine, back <= mine], axis=1)

    def of(q):
        scores = jnp.where(allowed, dot(q, all_keys, 1, 1) * scale, -1e30)
        weights = jnp.exp(scores - jnp.max(scores, axis=1, keepdims=True))
        return (weights * (1.0 / jnp.sum(weights, axis=1, keepdims=True))).astype(BF)

    return of


def prob_body(heads, scale, order, who, q, k, k_far, prob):
    hd = k.shape[1]
    of = probabilities(scale, order, who, k, k_far)
    for h in range(heads):
        prob[h] = of(q[:, h * hd : (h + 1) * hd])


def dval_body(heads, scale, order, who, q, g, k, k_far, near, far):
    rows, hd = k.shape
    of = probabilities(scale, order, who, k, k_far)
    total = jnp.zeros((2 * rows, hd), F32)
    for h in range(heads):
        cols = slice(h * hd, (h + 1) * hd)
        total += dot(of(q[:, cols]), g[:, cols], 0, 0)
    near[...] = total[:rows]
    far[...] = total[rows:].astype(BF)


def back_body(heads, scale, prob, q, g, k, k_far, v, v_far, attn, dq, near, far):
    rows, hd = k.shape
    all_keys = jnp.concatenate([k[...], k_far[...]], axis=0)
    all_values = jnp.concatenate([v[...], v_far[...]], axis=0)
    total = jnp.zeros((2 * rows, hd), F32)
    for h in range(heads):
        cols = slice(h * hd, (h + 1) * hd)
        p = prob[h]
        gh = g[:, cols]
        out = dot(p, all_values, 1, 0).astype(BF)
        attn[:, cols] = out
        delta = jnp.sum(gh.astype(F32) * out.astype(F32), axis=1, keepdims=True)
        ds = (p.astype(F32) * (dot(gh, all_values, 1, 1) - delta)).astype(BF)
        dq[:, cols] = (dot(ds, all_keys, 1, 0) * scale).astype(BF)
        total += dot(ds, q[:, cols], 0, 0)
    near[...] = total[:rows] * scale
    far[...] = (total[rows:] * scale).astype(BF)


def term_body(part, who, x, near, back, mine, theirs):
    dv = (near[...] + back[...].astype(F32)).astype(BF)
    first = who[2] == 0
    group = NC * NX * part
    step = 2 * group
    for j in range(x.shape[1] // step):
        t = dot(x[:, j * step : (j + 1) * step], dv, 0, 0)
        at = slice(2 * part * j, 2 * part * (j + 1))
        for quarter in range(NX):

            def rows_of(c):
                low = c * NX * part + quarter * part
                return jnp.concatenate([t[low : low + part], t[group + low : group + low + part]], axis=0)

            zero, one = rows_of(0), rows_of(1)
            mine[quarter, at] = jnp.where(first, zero, one).astype(BF)
            theirs[quarter, at] = jnp.where(first, one, zero).astype(BF)


def quarter_of(who, step, mine, theirs):
    at = lax.rem(who[3] + step, NX)
    return mine[at].astype(F32) + theirs[at].astype(F32)


def sides_body(who, mine, theirs, *outs):
    for step, out in enumerate(outs, 1):
        out[...] = quarter_of(who, step, mine, theirs).astype(BF)


def own_body(who, mine, theirs, *refs):
    total = quarter_of(who, 0, mine, theirs)
    for ref in refs[:-1]:
        total += ref[...].astype(F32)
    refs[-1][...] = total.astype(BF)


def sum_body(copies, parts, out):
    total = parts[0].astype(F32)
    for i in range(1, parts.shape[0]):
        total += parts[i].astype(F32)
    total = total.astype(out.dtype)
    if copies == 0:
        out[...] = total
    else:
        for i in range(copies):
            out[:, i] = total


def summed(parts, copies, kind=BF):
    shape = parts.shape[1:]
    if copies:
        shape = (shape[0], copies) + shape[1:]
    out = jax.ShapeDtypeStruct(shape, kind)
    return kernel(functools.partial(sum_body, copies), [VM], [out], parts.size)(parts)[0]


def gathered_weight(w):
    def everywhere(block, axis):
        count = lax.axis_size(axis)
        return exchanged(jnp.broadcast_to(block[None], (count,) + block.shape), axis)

    own = everywhere(w, "zl")
    mine = everywhere(own, "y").reshape((NY * NZ,) + w.shape)
    theirs = shifted(mine, "c", 1)
    first = lax.axis_index("c") == 0
    both = jnp.stack([jnp.where(first, mine, theirs), jnp.where(first, theirs, mine)], axis=1)
    return both.reshape(NY * NZ * NC * w.shape[0], w.shape[1])


def scattered_sum(who, x_rows, near, back, part):
    rows, width = x_rows.shape
    hd = near.shape[1]
    full = (NX, NY * NZ * part, hd)
    mine, theirs = kernel(
        functools.partial(term_body, part),
        [SM, VM, VM, VM],
        [jax.ShapeDtypeStruct(full, BF)] * 2,
        2 * rows * width * hd,
    )(who, x_rows, near, back)
    theirs = shifted(theirs, "c", 1)
    size = NY * NZ * part
    quarter = jax.ShapeDtypeStruct((size, hd), BF)
    sides = kernel(sides_body, [SM, VM, VM], [quarter] * 3, 3 * size * hd)(who, mine, theirs)
    got = []
    for step, side in zip((2, 1, 3), (sides[1], sides[0], sides[2])):
        got.append(shifted(side, "x", step))
    total = kernel(own_body, [SM] + [VM] * 5, [quarter], size * hd)(who, mine, theirs, *got)[0]
    total = total.reshape(NY, NZ, part, hd)
    got = exchanged(total, "y")
    total = summed(got, NH).reshape(NZ * NH, part, hd)
    got = exchanged(total, ("zl", "zh"))
    total = summed(got[:, None], NX, F32)[0]
    return exchanged(total, "x").reshape(NX * part, hd)


def shards(inputs, block_order, w_value, query, keys, out_grad):
    x_rows = inputs[0]
    q_rows = query[0]
    k_rows = keys[0]
    grad_rows = out_grad[0]
    rows, hd = k_rows.shape
    heads = q_rows.shape[1] // hd
    scale = 1.0 / hd**0.5
    index = lax.axis_index(CTX)
    count = lax.axis_size(CTX)
    who = jnp.stack([index, (index + count - 1) % count, lax.axis_index("c"), lax.axis_index("x")]).astype(jnp.int32)
    block = jax.ShapeDtypeStruct((rows, hd), F32)
    block_b = jax.ShapeDtypeStruct((rows, hd), BF)
    wide_b = jax.ShapeDtypeStruct(q_rows.shape, BF)
    work = 2 * rows * 2 * rows * hd * heads

    far_keys = shifted(k_rows, CTX, 1)
    w_full = gathered_weight(w_value)

    near, far = kernel(
        functools.partial(dval_body, heads, scale), [SM, SM] + [VM] * 4, [block, block_b], 4 * work
    )(in_hbm(block_order), who, in_hbm(q_rows), in_hbm(grad_rows), in_hbm(k_rows), far_keys)
    prob = kernel(
        functools.partial(prob_body, heads, scale),
        [SM, SM] + [VM] * 3,
        [jax.ShapeDtypeStruct((heads, rows, 2 * rows), BF)],
        2 * work,
    )(in_hbm(block_order), who, in_hbm(q_rows), in_hbm(k_rows), in_hbm(far_keys))[0]
    back = shifted(far, CTX, -1)
    grad_w = scattered_sum(who, x_rows, near, back, w_value.shape[0] // NX)

    values = jnp.dot(x_rows, w_full, preferred_element_type=F32).astype(BF)
    far_values = shifted(values, CTX, 1)
    attn, dquery, near_k, far_k = kernel(
        functools.partial(back_body, heads, scale),
        [VM] * 7,
        [wide_b, wide_b, block, block_b],
        6 * work,
    )(in_hbm(prob), in_hbm(q_rows), in_hbm(grad_rows), k_rows, far_keys, values, far_values)
    back_keys = shifted(far_k, CTX, -1).astype(F32)
    dkeys = (near_k + back_keys).astype(BF)
    return (attn[None], dquery[None], dkeys[None], grad_w)


def solution(mesh):
    fine = Mesh(mesh.devices.reshape(NY, NZ, NC, NX, NH), ("y", "zl", "c", "x", "zh"))
    return jax.shard_map(
        shards,
        mesh=fine,
        in_specs=(
            P(DP, CTX, None),
            P(),
            P(DP, None),
            P(DP, CTX, None),
            P(DP, CTX, None),
            P(DP, CTX, None),
        ),
        out_specs=(P(DP, CTX, None), P(DP, CTX, None), P(DP, CTX, None), P(DP, None)),
        check_vma=False,
    )
```
